256 devices in a mesh: tp: 8 (over y, z_hi), dp: 8 (over z_lo, core), hg: 4 (over x).
Axes of the slice: x: 4, y: 4, z: 8 (z_hi: 2, z_lo: 4; z = z_hi * 4 + z_lo), core: 2. Of those that a mesh axis runs over, the one named last changes fastest.
Arguments:
- hidden_in: bfloat16 [8, 4, 256, 4096], P('dp', 'hg', 'tp'), may hold values from -45 to 45
- norm_gain: float32 [4096], replicated, may hold values from 0.1 to 1.9
- qkv_weight: bfloat16 [4096, 3, 32, 128], P(('dp', 'hg'), None, 'tp'), may hold values from -0.09375 to 0.09375
- out_weight: bfloat16 [32, 128, 4096], P('tp', None, ('dp', 'hg')), may hold values from -0.5 to 0.5
- cache_kv: bfloat16 [8, 32, 1024, 256], P('dp', 'tp'), may hold values from -200 to 200
- cached_lengths: int32 [8], replicated, may hold values from 128 to 1024, as said below
- owner_table: int32 [8, 16], replicated, may hold values from 0 to 7, as said below
Outputs:
- hidden_out: bfloat16 [8, 4, 256, 4096], P('dp', 'hg', 'tp')
- decode_kv: bfloat16 [8, 32, 8, 2, 128, 256], P('dp', ('tp', 'hg'))
The draws below stay inside these ranges and needn't reach their ends.
Inputs may be any that keep to these rules, and one draw needn't show every extreme that they name: `cached_lengths`: multiples of 128; one request has exactly 1024. `owner_table`: a request has at most 2 valid blocks with one owner; one owner holds exactly 2 valid blocks of every request.
All inputs are finite; a program needn't handle non-finite values.
Results may differ from the reference program's by a relative error of at most 0.015.
Values may be sent and summed in bfloat16 or wider, within the bound.
A program may use at most 128 MiB of HBM per device.

```python
import math
import jax
import jax.numpy as jnp
from jax import lax

D = 4096
HEADS = 32
HD = 128
ROT = 32
STRETCH = 1024
PMAX = 1024
BLOCK = 128
REQS = 8
RUN = 256
NBLK = 16
CAP = 2
N_DP = 8
N_HG = 4


def draw_hidden_in(key, part):
    key_base, key_rows, key_cols = jax.random.split(key, 3)
    full_shape = (REQS, N_HG, RUN, D)
    row_scale = jnp.exp(jax.random.uniform(key_rows, (REQS, N_HG, RUN, 1), jnp.float32, -1.2, 1.2))
    col_scale = jnp.exp(jax.random.uniform(key_cols, (1, 1, 1, D), jnp.float32, -1.2, 1.2))
    base_draw = jnp.clip(jax.random.normal(key_base, full_shape, jnp.float32), -4.0, 4.0)
    return (base_draw * row_scale * col_scale).astype(jnp.bfloat16)


def draw_cache_kv(key, part):
    full_shape = (REQS, HEADS, PMAX, 2 * HD)
    key_base = jax.random.fold_in(key, 0)
    base_draw = jnp.clip(jax.random.normal(key_base, full_shape, jnp.float32), -6.0, 6.0)
    return base_draw.astype(jnp.bfloat16)


def lengths_and_owners(key):
    base_key = jax.random.fold_in(key, 11)
    key_exp, key_add, key_long, key_hot, key_rest = jax.random.split(base_key, 5)
    most_units = PMAX // BLOCK
    top_exp = most_units.bit_length() - 1
    powers = jnp.left_shift(jnp.ones((REQS,), jnp.int32), jax.random.randint(key_exp, (REQS,), 0, top_exp + 1))
    unit_count = jnp.minimum(powers + jax.random.randint(key_add, (REQS,), 0, powers), most_units)
    longest = jax.random.randint(key_long, (), 0, REQS)
    unit_count = jnp.where(jnp.arange(REQS, dtype=jnp.int32) == longest, most_units, unit_count).astype(jnp.int32)
    hot_owner = jax.random.randint(key_hot, (), 0, N_DP).astype(jnp.int32)

    def assign(request_key, used_blocks):
        key_order, key_perm = jax.random.split(request_key)
        block_ids = jnp.arange(NBLK, dtype=jnp.int32)
        shuffle = jax.random.permutation(key_order, NBLK).astype(jnp.int32)
        priority = jnp.where(block_ids < used_blocks, 0, NBLK) + shuffle
        ordering = jnp.argsort(priority, stable=True)
        position_rank = jnp.argsort(ordering, stable=True).astype(jnp.int32)
        owner_perm = jax.random.permutation(key_perm, N_DP).astype(jnp.int32)
        owner_perm = jnp.where(owner_perm == hot_owner, owner_perm[0], owner_perm)
        owner_perm = owner_perm.at[0].set(hot_owner)
        return owner_perm[position_rank // CAP]
    request_keys = jax.random.split(key_rest, REQS)
    owner_rows = jax.vmap(assign)(request_keys, unit_count + STRETCH // BLOCK)
    return ((unit_count * BLOCK).astype(jnp.int32), owner_rows.astype(jnp.int32))


def draw_cached_lengths(key, part):
    return lengths_and_owners(key)[0]


def draw_owner_table(key, part):
    return lengths_and_owners(key)[1]


def block_scale(stream_key, dims, cuts, low, high):
    def one(dim, blocks):
        draws = jax.random.uniform(jax.random.fold_in(jax.random.fold_in(stream_key, 6), dim), (blocks,), jnp.float32, low / len(cuts), high / len(cuts))
        return jnp.repeat(jnp.exp(draws), dims[dim] // blocks).reshape((-1,) + (1,) * (len(dims) - dim - 1))

    factor_of = one(*cuts[0])
    for cut in cuts[1:]:
        factor_of = factor_of * one(*cut)
    return factor_of


def normal_values(stream_key, shape, scale, bound, pieces=(), held_as=jnp.bfloat16):
    gain = block_scale(stream_key, shape, pieces, -0.22, 0.18) if pieces else 1.0
    drawn = jax.random.normal(stream_key, shape, jnp.float32) * scale * gain
    return jnp.minimum(jnp.maximum(drawn, -bound), bound).astype(held_as)


def setup_inputs(seed: int = 0) -> dict:
    keys = jax.random.split(jax.random.key(seed), 8)
    return {
        "hidden_in": draw_hidden_in(jax.random.fold_in(keys[7], 71), 0),
        "norm_gain": jnp.clip(1.0 + 0.18 * jax.random.normal(keys[1], (D,), jnp.float32), 0.1, 1.9),
        "qkv_weight": normal_values(keys[2], (D, 3, HEADS, HD), D ** -0.5, 0.09375, ((0, 32), (2, 8))),
        "out_weight": normal_values(keys[3], (HEADS, HD, D), HD ** -0.5, 0.5, ((0, 8), (2, 32))),
        "cache_kv": draw_cache_kv(jax.random.fold_in(keys[7], 71), 0),
        "cached_lengths": draw_cached_lengths(jax.random.fold_in(keys[7], 71), 0),
        "owner_table": draw_owner_table(jax.random.fold_in(keys[7], 71), 0),
    }


epsilon = 1e-05

def layer_norm(row_data, gain_row):
    row_data = row_data.astype(jnp.float32)
    centered = row_data - lax.optimization_barrier(jnp.mean(row_data, axis=-1, keepdims=True))
    spread = lax.optimization_barrier(jnp.mean(centered * centered, axis=-1, keepdims=True))
    return (centered * lax.rsqrt(spread + epsilon) * gain_row.astype(jnp.float32)).astype(jnp.bfloat16)

def rotate(vectors, positions, rot_dims):
    half_dims = rot_dims // 2
    frequency = 10000.0 ** (-2.0 * jnp.arange(half_dims, dtype=jnp.float32) / rot_dims)
    angles = positions.astype(jnp.float32)[:, None, None] * frequency[None, None, :]
    cosine = jnp.cos(angles)
    sine_part = jnp.sin(angles)
    first_half = vectors[..., :half_dims]
    second = vectors[..., half_dims:rot_dims]
    return jnp.concatenate([first_half * cosine - second * sine_part, second * cosine + first_half * sine_part, vectors[..., rot_dims:]], axis=-1)

def attend(queries, key_rows, value_rows, limit_base):
    scores = jnp.dot(queries, key_rows.T, preferred_element_type=jnp.float32) / math.sqrt(queries.shape[-1])
    row_limit = limit_base + jnp.arange(queries.shape[0], dtype=jnp.int32)
    allowed = jnp.arange(key_rows.shape[0], dtype=jnp.int32)[None, :] <= row_limit[:, None]
    scores = jnp.where(allowed, scores, -jnp.inf)
    row_max = lax.optimization_barrier(jnp.max(scores, axis=1, keepdims=True))
    weights = jnp.exp(scores - row_max)
    row_total = lax.optimization_barrier(jnp.sum(weights, axis=1, keepdims=True))
    attended = jnp.dot(weights.astype(jnp.bfloat16), value_rows, preferred_element_type=jnp.float32) / row_total
    return attended.astype(jnp.bfloat16)

def selector(owner_row, valid_end, low_block, high_block, owner_count, slot_cap):
    block_ids = jnp.arange(owner_row.shape[0], dtype=jnp.int32)
    is_valid = block_ids < valid_end
    same_owner = (owner_row[:, None] == owner_row[None, :]) & is_valid[None, :] & (block_ids[None, :] < block_ids[:, None])
    slot_rank = lax.optimization_barrier(jnp.sum(same_owner.astype(jnp.int32), axis=1))
    chosen = is_valid & (block_ids >= low_block) & (block_ids < high_block)
    slot_ids = jnp.arange(owner_count * slot_cap, dtype=jnp.int32)
    picked = chosen[None, :] & (owner_row[None, :] == (slot_ids // slot_cap)[:, None]) & (slot_rank[None, :] == (slot_ids % slot_cap)[:, None])
    return picked.astype(jnp.bfloat16)

def reference(hidden_in, norm_gain, qkv_weight, out_weight, cache_kv, cached_lengths, owner_table):
    head_width = HEADS * HD
    qkv_flat = qkv_weight.reshape(D, 3 * head_width)
    out_flat = out_weight.reshape(head_width, D)
    zero_index = jnp.zeros((), jnp.int32)
    outputs = []
    handed = []
    for request in range(REQS):
        length = cached_lengths[request]
        row_block = hidden_in[request].reshape(STRETCH, D)
        normed = layer_norm(row_block, norm_gain)
        projected = jnp.dot(normed, qkv_flat, preferred_element_type=jnp.float32)
        positions = length + jnp.arange(STRETCH, dtype=jnp.int32)
        queries = rotate(projected[:, :head_width].reshape(STRETCH, HEADS, HD), positions, ROT).astype(jnp.bfloat16)
        new_keys = rotate(projected[:, head_width:2 * head_width].reshape(STRETCH, HEADS, HD), positions, ROT).astype(jnp.bfloat16)
        new_values = projected[:, 2 * head_width:].reshape(STRETCH, HEADS, HD).astype(jnp.bfloat16)
        stretch_kv = jnp.concatenate([new_keys, new_values], axis=2).transpose(1, 0, 2)
        extended = jnp.concatenate([cache_kv[request], jnp.zeros((HEADS, STRETCH, 2 * HD), jnp.bfloat16)], axis=1)

        def one_head(operands):
            head_queries, head_extended, head_stretch = operands
            sequence = lax.dynamic_update_slice(head_extended, head_stretch, (length.astype(jnp.int32), zero_index))
            return (attend(head_queries, sequence[:, :HD], sequence[:, HD:], length), sequence)
        attended, sequence = lax.map(one_head, (queries.transpose(1, 0, 2), extended, stretch_kv))
        attn_sum = jnp.dot(attended.transpose(1, 0, 2).reshape(STRETCH, head_width), out_flat, preferred_element_type=jnp.float32)
        outputs.append((row_block.astype(jnp.float32) + attn_sum).astype(jnp.bfloat16).reshape(N_HG, RUN, D))
        valid_end = (length + STRETCH) // BLOCK
        picked = selector(owner_table[request], valid_end, 0, NBLK, N_DP, CAP)
        blocks = sequence.reshape(HEADS, NBLK, BLOCK * 2 * HD)
        placed = jnp.einsum('sb,hbx->shx', picked.astype(jnp.float32), blocks.astype(jnp.float32))
        handed.append(placed.astype(jnp.bfloat16).reshape(N_DP, CAP, HEADS, BLOCK, 2 * HD).transpose(0, 2, 1, 3, 4))
    return (jnp.stack(outputs), jnp.stack(handed, axis=2))
```

```python
import functools
import math

import jax
import jax.numpy as jnp
import numpy as np
from jax import lax
from jax.experimental import pallas as pl
from jax.experimental.pallas import tpu as pltpu
from jax.sharding import PartitionSpec as P

ROT = 32
BLOCK = 128
HD = 128
RUN = 256
ROWS = 32
D = 4096
PMAX = 1024
EPS = 1e-05
MESH = pl.DeviceIdType.MESH
BF = jnp.bfloat16
F32 = jnp.float32


def body(
    hid_ref, gain_ref, freq_ref, wq_ref, wo_ref, cache_ref, len_ref, own_ref,
    out_ref, dec_ref,
    abuf, wbuf, acc, tcos, tsin, wobuf, seq, qbuf, qsrc, kvsrc, asrc, atbuf,
    psum, rsum, zsrc, zbuf, fsrc, fbuf, hbuf, dsrc,
    a_ss, a_rs, sw_ss, sw_rs, w_zs, w_xs, w_hs, w_rs, loc,
    o_zs, o_xs, o_zr, o_xr, q_ss, q_rs, k_ss, k_rs, t_ss, t_rs,
    d_ss, d_rs, y_ss, y_rs, z_ss, z_rs, f_ss, f_rs, h_ss, h_rs,
):
    tp = lax.axis_index("tp")
    dp = lax.axis_index("dp")
    x = lax.axis_index("hg")
    y = tp // 2
    zh = tp % 2
    zl = dp // 2
    c = dp % 2

    def dev(x_=x, y_=y, zh_=zh, zl_=zl, c_=c):
        return {"tp": y_ * 2 + zh_, "dp": zl_ * 2 + c_, "hg": x_}

    def rcopy(src, dst, ss, rs, to):
        return pltpu.make_async_remote_copy(
            src_ref=src, dst_ref=dst, send_sem=ss, recv_sem=rs, device_id=to, device_id_type=MESH
        )

    here = dev()
    partner = dev(c_=1 - c)
    xp = dev(x_=(x + 1) % 4)
    xm = dev(x_=(x + 3) % 4)
    x2 = dev(x_=(x + 2) % 4)
    zup = dev(zl_=(zl + 1) % 4)
    zdn = dev(zl_=(zl + 3) % 4)
    zhp = dev(zh_=1 - zh)
    ys = [dev(y_=(y + i) % 4) for i in (1, 3, 2)]

    barrier = pltpu.get_barrier_semaphore()
    peers = [dev(x_=(x + i) % 4, c_=(c + j) % 2) for i in range(4) for j in range(2) if i or j]
    peers += [dev(zl_=(zl + i) % 4, c_=(c + j) % 2) for i in range(1, 4) for j in range(2)]
    peers += ys + [zhp]
    for to in peers:
        pl.semaphore_signal(barrier, inc=1, device_id=to, device_id_type=MESH)

    cache_cp = pltpu.make_async_copy(cache_ref.at[x], seq.at[pl.ds(0, 8)], loc.at[0])
    cache_cp.start()
    wown = wbuf.at[zl, x, pl.ds(c * 128, 128)]
    wcopy = pltpu.make_async_copy(wq_ref.at[c], wown, loc.at[1])
    wcopy.start()
    wocopy = pltpu.make_async_copy(
        wo_ref, wobuf.at[zl, :, pl.ds(pl.multiple_of(x * 128, 128), 128)], loc.at[2]
    )
    wocopy.start()
    rows = hid_ref[...].astype(F32)
    centered = rows - jnp.mean(rows, axis=-1, keepdims=True)
    spread = jnp.mean(centered * centered, axis=-1, keepdims=True)
    arow = lambda r, t: abuf.at[pl.ds(pl.multiple_of(r * RUN + t * ROWS, ROWS), ROWS)]
    abuf[pl.ds(pl.multiple_of(c * RUN + tp * ROWS, ROWS), ROWS), :] = (
        centered * lax.rsqrt(spread + EPS) * gain_ref[...]
    ).astype(BF)
    seq[16] = jnp.zeros((BLOCK, 256), BF)
    pl.semaphore_wait(barrier, len(peers))

    swap = rcopy(wq_ref.at[1 - c], wown, sw_ss, sw_rs, partner)
    swap.start()

    def acopy(r, t, i, to):
        return rcopy(arow(r, t), arow(r, t), a_ss.at[i], a_rs.at[r, t], to)

    a_sent = [acopy(c, tp, 0, zhp), acopy(c, tp, 1, partner)]
    a_sent += [acopy(c, tp, 2 + i, to) for i, to in enumerate(ys)]
    for cp in a_sent:
        cp.start()
    hswap = rcopy(hid_ref, hbuf, h_ss, h_rs, partner)
    hswap.start()

    def order(j):
        m = jnp.where(zl < 2, zl, 3 - zl)
        s = jnp.where((m == 1) & (j < 2), 1 - j, j)
        return jnp.where(zl < 2, s, 3 - s)

    up = lambda s: (s <= zl) & (zl < 3)
    down = lambda s: (s >= zl) & (zl > 0)

    def wz(s, i):
        return rcopy(wbuf.at[s, x], wbuf.at[s, x], w_zs.at[i, s], w_rs.at[s, 0], (zup, zdn)[i])

    def wx(s, i):
        return rcopy(
            wbuf.at[s, x], wbuf.at[s, x], w_xs.at[i, s], w_rs.at[s, 1 + i], (xp, xm)[i]
        )

    def wh(s, i):
        col = (x + 3 - 2 * i) % 4
        half = wbuf.at[s, col, pl.ds(i * 128, 128)]
        return rcopy(half, half, w_hs.at[i, s], w_rs.at[s, 3 + i], (xp, xm)[i])

    def oz(s, i):
        part = wobuf.at[s, :, pl.ds(pl.multiple_of(x * 128, 128), 128)]
        return rcopy(part, part, o_zs.at[i, s], o_zr.at[s], (zup, zdn)[i])

    def ox(s, i):
        part = wobuf.at[s, :, pl.ds(pl.multiple_of(x * 128, 128), 128)]
        return rcopy(part, part, o_xs.at[s, i], o_xr.at[s, i], (xp, xm, x2)[i])

    def relay(make, s):
        @pl.when(up(s))
        def _():
            make(s, 0).start()

        @pl.when(down(s))
        def _():
            make(s, 1).start()

    def step_own(j):
        s = order(j)
        if j:
            wz(s, 0).wait_recv()
        for i in range(2):
            wx(s, i).start()
        relay(wz, s)

    def step_near(j):
        s = order(j)
        for i in range(2):
            wx(s, i).wait_recv()
            wh(s, i).start()

    def project(s, col):
        k = s * 1024 + col * 128
        lhs = jnp.concatenate(
            [
                abuf[:, pl.ds(pl.multiple_of(k, 128), 128)],
                abuf[:, pl.ds(pl.multiple_of(k + 512, 128), 128)],
            ],
            axis=1,
        )
        acc[...] += jnp.dot(lhs, wbuf[s, col], preferred_element_type=F32)

    wcopy.wait()
    swap.wait_recv()
    step_own(0)

    iota = lax.broadcasted_iota(jnp.int32, (RUN, HD), 0)
    for r in range(2):
        pos = (len_ref[zl * 2 + r] + x * RUN + iota).astype(F32) * freq_ref[...]
        tcos[pl.ds(r * RUN, RUN), :] = jnp.cos(pos)
        tsin[pl.ds(r * RUN, RUN), :] = jnp.sin(pos)
    acc[...] = jnp.zeros_like(acc)

    a_fwd = []
    step_near(0)
    for i in range(3):
        t = ((y + (3, 1, 2)[i]) % 4) * 2 + zh
        cp = acopy(c, t, 5 + i, partner)
        cp.wait_recv()
        cp.start()
        a_fwd.append(cp)
    step_own(1)
    t = y * 2 + 1 - zh
    for i, to in enumerate(ys + [partner]):
        cp = acopy(c, t, 8 + i, to)
        if i == 0:
            cp.wait_recv()
        cp.start()
        a_fwd.append(cp)
    step_near(1)
    step_own(2)
    for i in range(3):
        t = ((y + (3, 1, 2)[i]) % 4) * 2 + 1 - zh
        cp = acopy(c, t, 12 + i, partner)
        cp.wait_recv()
        cp.start()
        a_fwd.append(cp)
    step_near(2)
    wocopy.wait()
    relay(oz, zl)
    step_own(3)
    for t in range(8):
        acopy(1 - c, t, 0, partner).wait_recv()

    def early(i, carry):
        j = i // 3
        s = order(j)
        project(s, (x + (i % 3) + 3) % 4)
        return carry

    lax.fori_loop(0, 9, early, 0)
    for j in (1, 2, 3):
        s = order(j)
        oz(s, 0).wait_recv()
        relay(oz, s)
    step_near(3)
    for j in range(4):
        s = order(j)
        for i in range(2):
            if j < 2:
                ox(s, i).start()
    for j in range(3):
        for i in range(2):
            wh_in = wbuf.at[order(j), (x + 2) % 4, pl.ds(i * 128, 128)]
            rcopy(wh_in, wh_in, w_hs.at[i, 0], w_rs.at[order(j), 3 + i], xp).wait_recv()

    def late(i, carry):
        s = order(jnp.where(i < 3, i, 3))
        project(s, jnp.where(i < 3, (x + 2) % 4, (x + i) % 4))
        return carry

    lax.fori_loop(0, 3, late, 0)
    lax.fori_loop(0, 3, lambda i, carry: (project(order(3), (x + i + 3) % 4), carry)[1], 0)
    for i in range(2):
        wh_in = wbuf.at[order(3), (x + 2) % 4, pl.ds(i * 128, 128)]
        rcopy(wh_in, wh_in, w_hs.at[i, 0], w_rs.at[order(3), 3 + i], xp).wait_recv()
    project(order(3), (x + 2) % 4)

    lane = lax.broadcasted_iota(jnp.int32, (RUN, HD), 1)

    def qcopies(h, r):
        to = dev(x_=2 * c + h, c_=r)
        i = h * 2 + r
        kdst = seq.at[pl.ds(8 + x * 2, 2)]
        return (
            rcopy(qsrc.at[h, r], qbuf.at[x], q_ss.at[i], q_rs.at[x], to),
            rcopy(kvsrc.at[h, r], kdst, k_ss.at[i], k_rs.at[x], to),
            pltpu.make_async_copy(qsrc.at[h, r], qbuf.at[x], q_rs.at[x]),
            pltpu.make_async_copy(kvsrc.at[h, r], kdst, k_rs.at[x]),
        )

    for r in range(2):
        sl = pl.ds(r * RUN, RUN)
        cos = tcos[sl, :]
        sin = tsin[sl, :]
        sin_a = jnp.where(lane < 16, -sin, 0.0)
        sin_b = jnp.where(lane < 16, 0.0, sin)

        def turn(v):
            return v * cos + pltpu.roll(v, HD - 16, 1) * sin_a + pltpu.roll(v, 16, 1) * sin_b

        for h in range(2):
            piece = lambda i: acc[sl, pl.ds((i * 2 + h) * HD, HD)]
            qsrc[h, r] = turn(piece(0)).astype(BF)
            kvsrc[h, r, :, :, pl.ds(0, HD)] = turn(piece(1)).astype(BF).reshape(2, BLOCK, HD)
            kvsrc[h, r, :, :, pl.ds(HD, HD)] = piece(2).astype(BF).reshape(2, BLOCK, HD)
            mine = (x == 2 * c + h) & (c == r)

            @pl.when(jnp.logical_not(mine))
            def _():
                cps = qcopies(h, r)
                cps[1].start()
                cps[0].start()

            @pl.when(mine)
            def _():
                cps = qcopies(h, r)
                cps[3].start()
                cps[2].start()

    length = len_ref[dp]
    cached = length // BLOCK
    valid_end = cached + 8
    owner = [own_ref[dp, b] for b in range(16)]
    rank = []
    for b in range(16):
        n = jnp.int32(0)
        for e in range(b):
            n += jnp.where((owner[e] == owner[b]) & (e < valid_end), 1, 0)
        rank.append(n)
    code = [
        jnp.where(b < valid_end, owner[b] * 2 + rank[b], -1) for b in range(16)
    ]
    source = [jnp.where(b < cached, b, 8 + b - cached) for b in range(16)]
    slots = []
    for s in range(16):
        n = jnp.int32(16)
        for b in range(16):
            n = jnp.where(code[b] == s, source[b], n)
        slots.append(n)

    cache_cp.wait()
    for i in range(4):
        pltpu.make_async_copy(qsrc.at[0, 0], qbuf.at[i], q_rs.at[i]).wait()
        pltpu.make_async_copy(
            kvsrc.at[0, 0], seq.at[pl.ds(8 + i * 2, 2)], k_rs.at[i]
        ).wait()

    def dcopies(o):
        to = {"tp": tp, "dp": o, "hg": x}
        return (
            rcopy(dsrc.at[o], dec_ref.at[dp], d_ss.at[o], d_rs.at[dp], to),
            pltpu.make_async_copy(dsrc.at[o], dec_ref.at[dp], d_rs.at[dp]),
        )

    for o in range(8):
        for k in range(2):
            dsrc[o, k] = seq[slots[o * 2 + k]]

        @pl.when(o != dp)
        def _():
            dcopies(o)[0].start()

        @pl.when(o == dp)
        def _():
            dcopies(o)[1].start()

    for j in range(4):
        s = order(j)
        for i in range(3):
            if j >= 2 or i == 2:
                ox(s, i).start()

    scale = 1.0 / math.sqrt(HD)

    def tcopies(g, k):
        to = dev(x_=g, c_=k)
        dst = atbuf.at[c, x]
        return (
            rcopy(asrc.at[g], dst, t_ss.at[g, k], t_rs.at[c, x], to),
            pltpu.make_async_copy(asrc.at[g], dst, t_rs.at[c, x]),
        )

    for g in (3, 2, 1, 0):
        n = PMAX + (g + 1) * RUN
        scores = (
            lax.dot_general(
                qbuf[g], seq[0 : n // BLOCK, :, 0:HD].reshape(n, HD), (((1,), (1,)), ((), ())),
                preferred_element_type=F32,
            )
            * scale
        )
        col = lax.broadcasted_iota(jnp.int32, (RUN, n), 1)
        row = lax.broadcasted_iota(jnp.int32, (RUN, n), 0)
        keep = (col < length) | ((col >= PMAX) & (col <= row + (PMAX + g * RUN)))
        scores = jnp.where(keep, scores, -jnp.inf)
        top = jnp.max(scores, axis=1, keepdims=True)
        weights = jnp.exp(scores - top)
        total = jnp.sum(weights, axis=1, keepdims=True)
        asrc[g] = (
            jnp.dot(
                weights.astype(BF),
                seq[0 : n // BLOCK, :, HD : 2 * HD].reshape(n, HD),
                preferred_element_type=F32,
            )
            / total
        ).astype(BF)
        for k in range(2):
            mine = (x == g) & (c == k)

            @pl.when(jnp.logical_not(mine))
            def _():
                tcopies(g, k)[0].start()

            @pl.when(mine)
            def _():
                tcopies(g, k)[1].start()

    for r in range(2):
        for h in range(4):
            pltpu.make_async_copy(asrc.at[0], atbuf.at[r, h], t_rs.at[r, h]).wait()
    lhs = jnp.concatenate(
        [jnp.concatenate([atbuf[r, h] for h in range(4)], axis=1) for r in range(2)], axis=0
    )

    def ycopy(q, i):
        to = (y + (1, 3, 2)[i]) % 4
        return rcopy(psum.at[q, to], rsum.at[q, i], y_ss.at[q, i], y_rs.at[q, i], ys[i])

    def zcopy(q):
        return rcopy(zsrc.at[q], zbuf.at[q], z_ss.at[q], z_rs.at[q], zhp)

    def fcopy(q):
        return rcopy(fsrc.at[q], fbuf.at[q], f_ss.at[q], f_rs.at[q], partner)

    for q in range(4):
        s = order(q)
        for i in range(3):
            ox(s, i).wait_recv()
        part = jnp.dot(lhs, wobuf[s], preferred_element_type=F32).astype(BF)
        for to in range(4):
            for r in range(2):
                psum[q, to, r] = part[r * RUN + to * 64 : r * RUN + to * 64 + 64]
        for i in (2, 0, 1):
            ycopy(q, i).start()
    sums = []
    for q in range(4):
        for i in range(3):
            ycopy(q, i).wait_recv()
        for r in range(2):
            far = pl.ds(pl.multiple_of((1 - zh) * ROWS, ROWS), ROWS)
            total = psum[q, y, r, far, :].astype(F32)
            for i in range(3):
                total += rsum[q, i, r, far, :].astype(F32)
            zsrc[q, r] = total.astype(BF)
        zcopy(q).start()
    near = pl.ds(pl.multiple_of(zh * ROWS, ROWS), ROWS)

    def total_of(q, r):
        total = psum[q, y, r, near, :].astype(F32)
        for i in range(3):
            total += rsum[q, i, r, near, :].astype(F32)
        return total + zbuf[q, r].astype(F32)

    for q in range(4):
        zcopy(q).wait_recv()
        if q == 0:
            hswap.wait_recv()
        cols = pl.ds(pl.multiple_of(order(q) * 1024 + c * 512, 512), 512)
        fsrc[q] = (hbuf[:, cols].astype(F32) + total_of(q, 1 - c)).astype(BF)
        fcopy(q).start()
        out_ref[:, cols] = (hid_ref[:, cols].astype(F32) + total_of(q, c)).astype(BF)
    for q in range(4):
        fcopy(q).wait_recv()
        cols = pl.ds(pl.multiple_of(order(q) * 1024 + (1 - c) * 512, 512), 512)
        out_ref[:, cols] = fbuf[q]

    for i in range(8):
        pltpu.make_async_copy(dsrc.at[0], dec_ref.at[i], d_rs.at[i]).wait()
    swap.wait_send()
    hswap.wait_send()
    for cp in a_sent + a_fwd:
        cp.wait_send()
    for j in range(4):
        for make in (wz, oz):

            @pl.when(up(j))
            def _():
                make(j, 0).wait_send()

            @pl.when(down(j))
            def _():
                make(j, 1).wait_send()

        for i in range(2):
            wx(j, i).wait_send()
            wh(j, i).wait_send()
        for i in range(3):
            ox(j, i).wait_send()
            ycopy(j, i).wait_send()
        zcopy(j).wait_send()
        fcopy(j).wait_send()
    for h in range(2):
        for r in range(2):

            @pl.when(jnp.logical_not((x == 2 * c + h) & (c == r)))
            def _():
                cps = qcopies(h, r)
                cps[0].wait_send()
                cps[1].wait_send()

    for g in range(4):
        for k in range(2):

            @pl.when(jnp.logical_not((x == g) & (c == k)))
            def _():
                tcopies(g, k)[0].wait_send()

    for o in range(8):

        @pl.when(o != dp)
        def _():
            dcopies(o)[0].wait_send()


def on_device(hidden_in, norm_gain, qkv_weight, out_weight, cache_kv, cached_lengths, owner_table):
    hid = hidden_in.reshape(ROWS, D)
    wq = (
        qkv_weight.reshape(128, 3, 2, 2, HD).transpose(2, 0, 1, 3, 4).reshape(2, 128, 6 * HD)
    )
    wo = out_weight.reshape(4 * HD, 128)
    cache = cache_kv.reshape(4, PMAX // BLOCK, BLOCK, 2 * HD)
    half = 10000.0 ** (-2.0 * np.arange(ROT // 2) / ROT)
    freq = np.zeros((1, HD), np.float32)
    freq[0, :ROT] = np.concatenate([half, half])
    vm = pl.BlockSpec(memory_space=pltpu.VMEM)
    sm = pl.BlockSpec(memory_space=pltpu.SMEM)
    hbm = pl.BlockSpec(memory_space=pl.ANY)
    dma = pltpu.SemaphoreType.DMA
    scratch = [
        pltpu.VMEM((512, D), BF),
        pltpu.VMEM((4, 4, 256, 768), BF),
        pltpu.VMEM((512, 768), F32),
        pltpu.VMEM((512, HD), F32),
        pltpu.VMEM((512, HD), F32),
        pltpu.VMEM((4, 512, 512), BF),
        pltpu.VMEM((17, BLOCK, 256), BF),
        pltpu.VMEM((4, RUN, HD), BF),
        pltpu.VMEM((2, 2, RUN, HD), BF),
        pltpu.VMEM((2, 2, 2, BLOCK, 2 * HD), BF),
        pltpu.VMEM((4, RUN, HD), BF),
        pltpu.VMEM((2, 4, RUN, HD), BF),
        pltpu.VMEM((4, 4, 2, 64, 512), BF),
        pltpu.VMEM((4, 3, 2, 64, 512), BF),
        pltpu.VMEM((4, 2, ROWS, 512), BF),
        pltpu.VMEM((4, 2, ROWS, 512), BF),
        pltpu.VMEM((4, ROWS, 512), BF),
        pltpu.VMEM((4, ROWS, 512), BF),
        pltpu.VMEM((ROWS, D), BF),
        pltpu.VMEM((8, 2, BLOCK, 256), BF),
        dma((15,)), dma((2, 8)), dma, dma, dma((2, 4)), dma((2, 4)), dma((2, 4)), dma((4, 5)),
        dma((3,)),
        dma((2, 4)), dma((4, 3)), dma((4,)), dma((4, 3)),
        dma((4,)), dma((4,)), dma((4,)), dma((4,)), dma((4, 2)), dma((2, 4)),
        dma((8,)), dma((8,)), dma((4, 3)), dma((4, 3)), dma((4,)), dma((4,)),
        dma((4,)), dma((4,)), dma, dma,
    ]
    out, dec = pl.pallas_call(
        body,
        name="branch",
        out_shape=(
            jax.ShapeDtypeStruct((ROWS, D), BF),
            jax.ShapeDtypeStruct((8, 2, BLOCK, 2 * HD), BF),
        ),
        in_specs=[vm, vm, vm, vm, vm, hbm, sm, sm],
        out_specs=(vm, hbm),
        scratch_shapes=scratch,
        compiler_params=pltpu.CompilerParams(
            collective_id=0, has_side_effects=True, vmem_limit_bytes=60 * 1024 * 1024
        ),
    )(hid, norm_gain.reshape(1, D), jnp.asarray(freq), wq, wo, cache, cached_lengths, owner_table)
    return out.reshape(hidden_in.shape), dec.reshape(1, 1, 8, 2, BLOCK, 2 * HD)


def solution(mesh):
    return jax.shard_map(
        on_device,
        mesh=mesh,
        in_specs=(
            P("dp", "hg", "tp", None),
            P(),
            P(("dp", "hg"), None, "tp", None),
            P("tp", None, ("dp", "hg")),
            P("dp", "tp", None, None),
            P(),
            P(),
        ),
        out_specs=(P("dp", "hg", "tp", None), P("dp", ("tp", "hg"), None, None, None, None)),
        check_vma=False,
    )
```

```python
import functools
import math

import jax
import jax.numpy as jnp
import numpy as np
from jax import lax
from jax.experimental import pallas as pl
from jax.experimental.pallas import tpu as pltpu
from jax.sharding import PartitionSpec as P

ROT = 32
BLOCK = 128
HD = 128
RUN = 256
ROWS = 32
D = 4096
PMAX = 1024
EPS = 1e-05
MESH = pl.DeviceIdType.MESH
BF = jnp.bfloat16
F32 = jnp.float32


def body(
    hid_ref, gain_ref, freq_ref, wq_ref, wo_ref, cache_ref, len_ref, own_ref,
    out_ref, dec_ref,
    abuf, wbuf, acc, tcos, tsin, wobuf, seq, qbuf, qsrc, kvsrc, asrc, atbuf,
    psum, rbuf, rsrc, zsrc, zbuf, fsrc, fbuf, dsrc,
    a_ss, a_rs, sw_ss, sw_rs, w_zs, w_xs, w_hs, w_rs, loc,
    o_zs, o_xs, o_zr, o_xr, q_ss, q_rs, k_ss, k_rs, t_ss, t_rs,
    d_ss, d_rs, y_ss, y_rs, z_ss, z_rs, f_ss, f_rs,
):
    tp = lax.axis_index("tp")
    dp = lax.axis_index("dp")
    x = lax.axis_index("hg")
    y = tp // 2
    zh = tp % 2
    zl = dp // 2
    c = dp % 2

    def dev(x_=x, y_=y, zh_=zh, zl_=zl, c_=c):
        return {"tp": y_ * 2 + zh_, "dp": zl_ * 2 + c_, "hg": x_}

    def rcopy(src, dst, ss, rs, to):
        return pltpu.make_async_remote_copy(
            src_ref=src, dst_ref=dst, send_sem=ss, recv_sem=rs, device_id=to, device_id_type=MESH
        )

    here = dev()
    partner = dev(c_=1 - c)
    xp = dev(x_=(x + 1) % 4)
    xm = dev(x_=(x + 3) % 4)
    x2 = dev(x_=(x + 2) % 4)
    zup = dev(zl_=(zl + 1) % 4)
    zdn = dev(zl_=(zl + 3) % 4)
    zhp = dev(zh_=1 - zh)
    zhq = dev(zh_=1 - zh, c_=1 - c)
    ys = [dev(y_=(y + i) % 4) for i in (1, 3, 2)]

    barrier = pltpu.get_barrier_semaphore()
    peers = [dev(x_=(x + i) % 4, c_=(c + j) % 2) for i in range(4) for j in range(2) if i or j]
    peers += [dev(zl_=(zl + i) % 4, c_=(c + j) % 2) for i in range(1, 4) for j in range(2)]
    peers += ys + [zhp, zhq]
    for to in peers:
        pl.semaphore_signal(barrier, inc=1, device_id=to, device_id_type=MESH)

    cache_cp = pltpu.make_async_copy(cache_ref.at[x], seq.at[pl.ds(0, 8)], loc.at[0])
    cache_cp.start()
    wown = wbuf.at[zl, x, pl.ds(c * 128, 128)]
    wcopy = pltpu.make_async_copy(wq_ref.at[c], wown, loc.at[1])
    wcopy.start()
    wocopy = pltpu.make_async_copy(
        wo_ref, wobuf.at[zl, :, pl.ds(pl.multiple_of(x * 128, 128), 128)], loc.at[2]
    )
    wocopy.start()
    rows = hid_ref[...].astype(F32)
    centered = rows - jnp.mean(rows, axis=-1, keepdims=True)
    spread = jnp.mean(centered * centered, axis=-1, keepdims=True)
    arow = lambda r, t: abuf.at[pl.ds(pl.multiple_of(r * RUN + t * ROWS, ROWS), ROWS)]
    abuf[pl.ds(pl.multiple_of(c * RUN + tp * ROWS, ROWS), ROWS), :] = (
        centered * lax.rsqrt(spread + EPS) * gain_ref[...]
    ).astype(BF)
    seq[16] = jnp.zeros((BLOCK, 256), BF)
    pl.semaphore_wait(barrier, len(peers))

    swap = rcopy(wq_ref.at[1 - c], wown, sw_ss, sw_rs, partner)
    swap.start()

    def acopy(r, t, i, to):
        return rcopy(arow(r, t), arow(r, t), a_ss.at[i], a_rs.at[r, t], to)

    a_sent = [acopy(c, tp, 0, zhp), acopy(c, tp, 1, partner)]
    a_sent += [acopy(c, tp, 2 + i, to) for i, to in enumerate(ys)]
    for cp in a_sent:
        cp.start()

    def order(j):
        m = jnp.where(zl < 2, zl, 3 - zl)
        s = jnp.where((m == 1) & (j < 2), 1 - j, j)
        return jnp.where(zl < 2, s, 3 - s)

    up = lambda s: (s <= zl) & (zl < 3)
    down = lambda s: (s >= zl) & (zl > 0)

    def wz(s, i):
        return rcopy(wbuf.at[s, x], wbuf.at[s, x], w_zs.at[i, s], w_rs.at[s, 0], (zup, zdn)[i])

    def wx(s, i):
        return rcopy(
            wbuf.at[s, x], wbuf.at[s, x], w_xs.at[i, s], w_rs.at[s, 1 + i], (xp, xm)[i]
        )

    def wh(s, i):
        col = (x + 3 - 2 * i) % 4
        half = wbuf.at[s, col, pl.ds(i * 128, 128)]
        return rcopy(half, half, w_hs.at[i, s], w_rs.at[s, 3 + i], (xp, xm)[i])

    def oz(s, i):
        return rcopy(wobuf.at[s], wobuf.at[s], o_zs.at[i, s], o_zr.at[s], (zup, zdn)[i])

    def ox(i):
        part = wobuf.at[zl, :, pl.ds(pl.multiple_of(x * 128, 128), 128)]
        return rcopy(wo_ref, part, o_xs.at[i], o_xr.at[i], (xp, xm, x2)[i])

    def relay(make, s):
        @pl.when(up(s))
        def _():
            make(s, 0).start()

        @pl.when(down(s))
        def _():
            make(s, 1).start()

    def step_own(j):
        s = order(j)
        if j:
            wz(s, 0).wait_recv()
        for i in range(2):
            wx(s, i).start()
        relay(wz, s)

    def step_near(j):
        s = order(j)
        for i in range(2):
            wx(s, i).wait_recv()
            wh(s, i).start()

    def project(s, col):
        k = s * 1024 + col * 128
        lhs = jnp.concatenate(
            [
                abuf[:, pl.ds(pl.multiple_of(k, 128), 128)],
                abuf[:, pl.ds(pl.multiple_of(k + 512, 128), 128)],
            ],
            axis=1,
        )
        acc[...] += jnp.dot(lhs, wbuf[s, col], preferred_element_type=F32)

    wcopy.wait()
    swap.wait_recv()
    step_own(0)
    for i in range(3):
        ox(i).start()

    iota = lax.broadcasted_iota(jnp.int32, (RUN, HD), 0)
    for r in range(2):
        pos = (len_ref[zl * 2 + r] + x * RUN + iota).astype(F32) * freq_ref[...]
        tcos[pl.ds(r * RUN, RUN), :] = jnp.cos(pos)
        tsin[pl.ds(r * RUN, RUN), :] = jnp.sin(pos)
    acc[...] = jnp.zeros_like(acc)

    a_fwd = []
    step_near(0)
    for i in range(3):
        t = ((y + (3, 1, 2)[i]) % 4) * 2 + zh
        cp = acopy(c, t, 5 + i, partner)
        cp.wait_recv()
        cp.start()
        a_fwd.append(cp)
    step_own(1)
    t = y * 2 + 1 - zh
    for i, to in enumerate(ys + [partner]):
        cp = acopy(c, t, 8 + i, to)
        if i == 0:
            cp.wait_recv()
        cp.start()
        a_fwd.append(cp)
    step_near(1)
    step_own(2)
    for i in range(3):
        t = ((y + (3, 1, 2)[i]) % 4) * 2 + 1 - zh
        cp = acopy(c, t, 12 + i, partner)
        cp.wait_recv()
        cp.start()
        a_fwd.append(cp)
    step_near(2)
    step_own(3)
    wocopy.wait()
    for i in range(3):
        ox(i).wait_recv()
    relay(oz, zl)
    for t in range(8):
        acopy(1 - c, t, 0, partner).wait_recv()

    def early(i, carry):
        j = i // 3
        s = order(j)
        project(s, (x + (i % 3) + 3) % 4)
        return carry

    lax.fori_loop(0, 9, early, 0)
    middle = (zl == 1) | (zl == 2)

    @pl.when(middle)
    def _():
        for j in (1, 2):
            oz(order(j), 0).wait_recv()
            relay(oz, order(j))

    step_near(3)
    for j in range(3):
        for i in range(2):
            wh_in = wbuf.at[order(j), (x + 2) % 4, pl.ds(i * 128, 128)]
            rcopy(wh_in, wh_in, w_hs.at[i, 0], w_rs.at[order(j), 3 + i], xp).wait_recv()

    def late(i, carry):
        s = order(jnp.where(i < 3, i, 3))
        project(s, jnp.where(i < 3, (x + 2) % 4, (x + i) % 4))
        return carry

    lax.fori_loop(0, 3, late, 0)
    lax.fori_loop(0, 3, lambda i, carry: (project(order(3), (x + i + 3) % 4), carry)[1], 0)
    for i in range(2):
        wh_in = wbuf.at[order(3), (x + 2) % 4, pl.ds(i * 128, 128)]
        rcopy(wh_in, wh_in, w_hs.at[i, 0], w_rs.at[order(3), 3 + i], xp).wait_recv()
    project(order(3), (x + 2) % 4)

    lane = lax.broadcasted_iota(jnp.int32, (RUN, HD), 1)

    def qcopies(h, r):
        to = dev(x_=2 * c + h, c_=r)
        i = h * 2 + r
        kdst = seq.at[pl.ds(8 + x * 2, 2)]
        return (
            rcopy(qsrc.at[h, r], qbuf.at[x], q_ss.at[i], q_rs.at[x], to),
            rcopy(kvsrc.at[h, r], kdst, k_ss.at[i], k_rs.at[x], to),
            pltpu.make_async_copy(qsrc.at[h, r], qbuf.at[x], q_rs.at[x]),
            pltpu.make_async_copy(kvsrc.at[h, r], kdst, k_rs.at[x]),
        )

    for r in range(2):
        sl = pl.ds(r * RUN, RUN)
        cos = tcos[sl, :]
        sin = tsin[sl, :]
        sin_a = jnp.where(lane < 16, -sin, 0.0)
        sin_b = jnp.where(lane < 16, 0.0, sin)

        def turn(v):
            return v * cos + pltpu.roll(v, HD - 16, 1) * sin_a + pltpu.roll(v, 16, 1) * sin_b

        for h in range(2):
            piece = lambda i: acc[sl, pl.ds((i * 2 + h) * HD, HD)]
            qsrc[h, r] = turn(piece(0)).astype(BF)
            kvsrc[h, r, :, :, pl.ds(0, HD)] = turn(piece(1)).astype(BF).reshape(2, BLOCK, HD)
            kvsrc[h, r, :, :, pl.ds(HD, HD)] = piece(2).astype(BF).reshape(2, BLOCK, HD)
            mine = (x == 2 * c + h) & (c == r)

            @pl.when(jnp.logical_not(mine))
            def _():
                cps = qcopies(h, r)
                cps[1].start()
                cps[0].start()

            @pl.when(mine)
            def _():
                cps = qcopies(h, r)
                cps[3].start()
                cps[2].start()

    @pl.when(middle)
    def _():
        oz(order(3), 0).wait_recv()
        relay(oz, order(3))

    length = len_ref[dp]
    cached = length // BLOCK
    valid_end = cached + 8
    owner = [own_ref[dp, b] for b in range(16)]
    rank = []
    for b in range(16):
        n = jnp.int32(0)
        for e in range(b):
            n += jnp.where((owner[e] == owner[b]) & (e < valid_end), 1, 0)
        rank.append(n)
    code = [
        jnp.where(b < valid_end, owner[b] * 2 + rank[b], -1) for b in range(16)
    ]
    source = [jnp.where(b < cached, b, 8 + b - cached) for b in range(16)]
    slots = []
    for s in range(16):
        n = jnp.int32(16)
        for b in range(16):
            n = jnp.where(code[b] == s, source[b], n)
        slots.append(n)

    cache_cp.wait()
    for i in range(4):
        pltpu.make_async_copy(qsrc.at[0, 0], qbuf.at[i], q_rs.at[i]).wait()
        pltpu.make_async_copy(
            kvsrc.at[0, 0], seq.at[pl.ds(8 + i * 2, 2)], k_rs.at[i]
        ).wait()

    def dcopies(o):
        to = {"tp": tp, "dp": o, "hg": x}
        return (
            rcopy(dsrc.at[o], dec_ref.at[dp], d_ss.at[o], d_rs.at[dp], to),
            pltpu.make_async_copy(dsrc.at[o], dec_ref.at[dp], d_rs.at[dp]),
        )

    for o in range(8):
        for k in range(2):
            dsrc[o, k] = seq[slots[o * 2 + k]]

        @pl.when(o != dp)
        def _():
            dcopies(o)[0].start()

        @pl.when(o == dp)
        def _():
            dcopies(o)[1].start()

    scale = 1.0 / math.sqrt(HD)

    def tcopies(g, k):
        to = dev(x_=g, c_=k)
        dst = atbuf.at[c, x]
        return (
            rcopy(asrc.at[g], dst, t_ss.at[g, k], t_rs.at[c, x], to),
            pltpu.make_async_copy(asrc.at[g], dst, t_rs.at[c, x]),
        )

    for g in (3, 2, 1, 0):
        n = PMAX + (g + 1) * RUN
        scores = (
            lax.dot_general(
                qbuf[g], seq[0 : n // BLOCK, :, 0:HD].reshape(n, HD), (((1,), (1,)), ((), ())),
                preferred_element_type=F32,
            )
            * scale
        )
        col = lax.broadcasted_iota(jnp.int32, (RUN, n), 1)
        row = lax.broadcasted_iota(jnp.int32, (RUN, n), 0)
        keep = (col < length) | ((col >= PMAX) & (col <= row + (PMAX + g * RUN)))
        scores = jnp.where(keep, scores, -jnp.inf)
        top = jnp.max(scores, axis=1, keepdims=True)
        weights = jnp.exp(scores - top)
        total = jnp.sum(weights, axis=1, keepdims=True)
        asrc[g] = (
            jnp.dot(
                weights.astype(BF),
                seq[0 : n // BLOCK, :, HD : 2 * HD].reshape(n, HD),
                preferred_element_type=F32,
            )
            / total
        ).astype(BF)
        for k in range(2):
            mine = (x == g) & (c == k)

            @pl.when(jnp.logical_not(mine))
            def _():
                tcopies(g, k)[0].start()

            @pl.when(mine)
            def _():
                tcopies(g, k)[1].start()

    for r in range(2):
        for h in range(4):
            pltpu.make_async_copy(asrc.at[0], atbuf.at[r, h], t_rs.at[r, h]).wait()
    lhs = jnp.concatenate(
        [jnp.concatenate([atbuf[r, h] for h in range(4)], axis=1) for r in range(2)], axis=0
    )

    yp = (y + 1) % 4
    ym = (y + 3) % 4
    yf = (y + 2) % 4

    def ycopy(q, i):
        src = (
            psum.at[q, yf, 0], psum.at[q, yf, 1], psum.at[q, yp, 1], psum.at[q, ym, 0],
            rsrc.at[q, 0], rsrc.at[q, 1],
        )[i]
        return rcopy(src, rbuf.at[q, i], y_ss.at[q, i], y_rs.at[q, i], ys[i % 2])

    def zcopy(q, r):
        to = dev(zh_=1 - zh, c_=r)
        return rcopy(zsrc.at[q, r], zbuf.at[q, c], z_ss.at[q, r], z_rs.at[q, c], to)

    def fcopy(q):
        return rcopy(fsrc.at[q], fbuf.at[q], f_ss.at[q], f_rs.at[q], partner)

    def add_far(q):
        for i, to in enumerate((yp, ym)):
            ycopy(q, i).wait_recv()
            rsrc[q, i] = (psum[q, to, i].astype(F32) + rbuf[q, i].astype(F32)).astype(BF)
            ycopy(q, 4 + i).start()

    for q in range(4):
        s = order(q)
        if q:

            @pl.when(jnp.logical_not(middle))
            def _():
                oz(s, 0).wait_recv()

        part = jnp.dot(lhs, wobuf[s], preferred_element_type=F32).astype(BF)
        for i in range(2):
            for to in range(4):
                for r in range(2):
                    psum[q, to, i, r] = part[
                        r * RUN + to * 64 : r * RUN + to * 64 + 64, i * 256 : i * 256 + 256
                    ]
        for i in range(4):
            ycopy(q, i).start()
        if q > 1:
            add_far(q - 2)
    for q in (2, 3):
        add_far(q)
    far = pl.ds(pl.multiple_of((1 - zh) * ROWS, ROWS), ROWS)
    near = pl.ds(pl.multiple_of(zh * ROWS, ROWS), ROWS)

    def total_of(q, r, rows):
        a, b = (
            psum[q, y, i, r, rows, :].astype(F32)
            + rbuf[q, 3 - i, r, rows, :].astype(F32)
            + rbuf[q, 4 + i, r, rows, :].astype(F32)
            for i in range(2)
        )
        return jnp.concatenate([a, b], axis=1)

    for q in range(4):
        for i in range(2, 6):
            ycopy(q, i).wait_recv()
        for r in range(2):
            zsrc[q, r] = total_of(q, r, far).astype(BF)
            zcopy(q, r).start()
        fsrc[q] = total_of(q, 1 - c, near).astype(BF)
        fcopy(q).start()
    for q in range(4):
        fcopy(q).wait_recv()
        for k in range(2):
            pltpu.make_async_copy(zsrc.at[0, 0], zbuf.at[q, k], z_rs.at[q, k]).wait()
        base = order(q) * 1024
        cols = pl.ds(pl.multiple_of(base + c * 512, 512), 512)
        total = total_of(q, c, near) + zbuf[q, c].astype(F32)
        out_ref[:, cols] = (hid_ref[:, cols].astype(F32) + total).astype(BF)
        cols = pl.ds(pl.multiple_of(base + (1 - c) * 512, 512), 512)
        total = fbuf[q].astype(F32) + zbuf[q, 1 - c].astype(F32)
        out_ref[:, cols] = (hid_ref[:, cols].astype(F32) + total).astype(BF)

    for i in range(8):
        pltpu.make_async_copy(dsrc.at[0], dec_ref.at[i], d_rs.at[i]).wait()
    swap.wait_send()
    for i in range(3):
        ox(i).wait_send()
    for cp in a_sent + a_fwd:
        cp.wait_send()
    for j in range(4):
        for make in (wz, oz):

            @pl.when(up(j))
            def _():
                make(j, 0).wait_send()

            @pl.when(down(j))
            def _():
                make(j, 1).wait_send()

        for i in range(2):
            wx(j, i).wait_send()
            wh(j, i).wait_send()
        for i in range(6):
            ycopy(j, i).wait_send()
        for r in range(2):
            zcopy(j, r).wait_send()
        fcopy(j).wait_send()
    for h in range(2):
        for r in range(2):

            @pl.when(jnp.logical_not((x == 2 * c + h) & (c == r)))
            def _():
                cps = qcopies(h, r)
                cps[0].wait_send()
                cps[1].wait_send()

    for g in range(4):
        for k in range(2):

            @pl.when(jnp.logical_not((x == g) & (c == k)))
            def _():
                tcopies(g, k)[0].wait_send()

    for o in range(8):

        @pl.when(o != dp)
        def _():
            dcopies(o)[0].wait_send()


def on_device(hidden_in, norm_gain, qkv_weight, out_weight, cache_kv, cached_lengths, owner_table):
    hid = hidden_in.reshape(ROWS, D)
    wq = (
        qkv_weight.reshape(128, 3, 2, 2, HD).transpose(2, 0, 1, 3, 4).reshape(2, 128, 6 * HD)
    )
    wo = out_weight.reshape(4 * HD, 128)
    cache = cache_kv.reshape(4, PMAX // BLOCK, BLOCK, 2 * HD)
    half = 10000.0 ** (-2.0 * np.arange(ROT // 2) / ROT)
    freq = np.zeros((1, HD), np.float32)
    freq[0, :ROT] = np.concatenate([half, half])
    vm = pl.BlockSpec(memory_space=pltpu.VMEM)
    sm = pl.BlockSpec(memory_space=pltpu.SMEM)
    hbm = pl.BlockSpec(memory_space=pl.ANY)
    dma = pltpu.SemaphoreType.DMA
    scratch = [
        pltpu.VMEM((512, D), BF),
        pltpu.VMEM((4, 4, 256, 768), BF),
        pltpu.VMEM((512, 768), F32),
        pltpu.VMEM((512, HD), F32),
        pltpu.VMEM((512, HD), F32),
        pltpu.VMEM((4, 512, 512), BF),
        pltpu.VMEM((17, BLOCK, 256), BF),
        pltpu.VMEM((4, RUN, HD), BF),
        pltpu.VMEM((2, 2, RUN, HD), BF),
        pltpu.VMEM((2, 2, 2, BLOCK, 2 * HD), BF),
        pltpu.VMEM((4, RUN, HD), BF),
        pltpu.VMEM((2, 4, RUN, HD), BF),
        pltpu.VMEM((4, 4, 2, 2, 64, 256), BF),
        pltpu.VMEM((4, 6, 2, 64, 256), BF),
        pltpu.VMEM((4, 2, 2, 64, 256), BF),
        pltpu.VMEM((4, 2, ROWS, 512), BF),
        pltpu.VMEM((4, 2, ROWS, 512), BF),
        pltpu.VMEM((4, ROWS, 512), BF),
        pltpu.VMEM((4, ROWS, 512), BF),
        pltpu.VMEM((8, 2, BLOCK, 256), BF),
        dma((15,)), dma((2, 8)), dma, dma, dma((2, 4)), dma((2, 4)), dma((2, 4)), dma((4, 5)),
        dma((3,)),
        dma((2, 4)), dma((3,)), dma((4,)), dma((3,)),
        dma((4,)), dma((4,)), dma((4,)), dma((4,)), dma((4, 2)), dma((2, 4)),
        dma((8,)), dma((8,)), dma((4, 6)), dma((4, 6)), dma((4, 2)), dma((4, 2)),
        dma((4,)), dma((4,)),
    ]
    out, dec = pl.pallas_call(
        body,
        name="branch",
        out_shape=(
            jax.ShapeDtypeStruct((ROWS, D), BF),
            jax.ShapeDtypeStruct((8, 2, BLOCK, 2 * HD), BF),
        ),
        in_specs=[vm, vm, vm, vm, vm, hbm, sm, sm],
        out_specs=(vm, hbm),
        scratch_shapes=scratch,
        compiler_params=pltpu.CompilerParams(
            collective_id=0, has_side_effects=True, vmem_limit_bytes=60 * 1024 * 1024
        ),
    )(hid, norm_gain.reshape(1, D), jnp.asarray(freq), wq, wo, cache, cached_lengths, owner_table)
    return out.reshape(hidden_in.shape), dec.reshape(1, 1, 8, 2, BLOCK, 2 * HD)


def solution(mesh):
    return jax.shard_map(
        on_device,
        mesh=mesh,
        in_specs=(
            P("dp", "hg", "tp", None),
            P(),
            P(("dp", "hg"), None, "tp", None),
            P("tp", None, ("dp", "hg")),
            P("dp", "tp", None, None),
            P(),
            P(),
        ),
        out_specs=(P("dp", "hg", "tp", None), P("dp", ("tp", "hg"), None, None, None, None)),
        check_vma=False,
    )
```
